32 devices in a mesh: span: 8 (over z, y), cross: 4 (over x, core).
Axes of the slice: x: 2, y: 2, z: 4, core: 2. Of those that a mesh axis runs over, the one named last changes fastest.
Arguments:
- divergence: float32 [64, 128, 256], P('span', 'cross'), may hold values from -6 to 6
- inverse_density: float32 [64, 128, 256], P('span', 'cross'), may hold values from 0.5 to 2
Outputs:
- pressure: float32 [64, 128, 256], P('span', 'cross')
- residual: float32 [64, 128, 256], P('span', 'cross')
The draws below stay inside these ranges and needn't reach their ends.
All inputs are finite; a program needn't handle non-finite values.
Results may differ from the reference program's by a relative error of at most 0.0002.
Values sent between devices are 32-bit elements; how exact they have to be, the bound alone decides.
A program may use at most 64 MiB of HBM per device.

```python
import math
import jax
import jax.numpy as jnp
from jax import lax

ITERS_C = 64
NX = 64
NY = 128
NZ = 256


def draw_divergence(key, part):
    along_x = jnp.sin(jnp.pi * (jnp.arange(NX, dtype=jnp.float32) + 0.5) / NX)
    along_y = jnp.sin(jnp.pi * (jnp.arange(NY, dtype=jnp.float32) + 0.5) / NY)
    along_z = jnp.sin(jnp.pi * (jnp.arange(NZ, dtype=jnp.float32) + 0.5) / NZ)
    smooth = along_x[:, None, None] * along_y[None, :, None] * along_z[None, None, :]
    rough = jnp.clip(jax.random.normal(key, (NX, NY, NZ), jnp.float32), -4.0, 4.0)
    return rough + 1.5 * smooth


def shard_levels(rng, extent, pieces, low, high):
    level, own = 1.0, jax.random.fold_in(rng, 6)
    for position, shards_of in pieces:
        heights = jnp.exp(jax.random.uniform(jax.random.fold_in(own, position), (shards_of,), jnp.float32, low / len(pieces), high / len(pieces)))
        level = level * jnp.repeat(heights, extent[position] // shards_of).reshape([-1 if axis == position else 1 for axis in range(len(extent))])
    return level


def setup_inputs(seed: int = 0) -> dict:
    seeds = jax.random.split(jax.random.key(seed), 3)
    divergence = draw_divergence(jax.random.fold_in(seeds[2], 71), 0)
    inverse_density = jnp.clip(jnp.exp(math.log(2.0) - 1.3862944 * jax.random.uniform(seeds[1], (NX, NY, NZ), jnp.float32) ** shard_levels(seeds[1], (NX, NY, NZ), ((0, 8), (1, 4)), -0.2, 0.2)), 0.5, 2.0)
    return dict(divergence=divergence, inverse_density=inverse_density)


RELAX = 0.8


def widen_global(field):
    return jnp.pad(field, 1)


def face_means(padded):
    face_x = 0.5 * (padded[1:, 1:-1, 1:-1] + padded[:-1, 1:-1, 1:-1])
    face_y = 0.5 * (padded[1:-1, 1:, 1:-1] + padded[1:-1, :-1, 1:-1])
    face_z = 0.5 * (padded[1:-1, 1:-1, 1:] + padded[1:-1, 1:-1, :-1])
    return face_x, face_y, face_z


def level_setup(conduct, scale, widen):
    face_x, face_y, face_z = face_means(widen(conduct))
    total = face_x[1:] + face_x[:-1] + face_y[:, 1:] + face_y[:, :-1] + face_z[:, :, 1:] + face_z[:, :, :-1]
    return face_x, face_y, face_z, scale * total


def apply_operator(padded, level, scale):
    face_x, face_y, face_z = level[0], level[1], level[2]
    centre = padded[1:-1, 1:-1, 1:-1]
    flux = face_x[1:] * (centre - padded[2:, 1:-1, 1:-1]) + face_x[:-1] * (centre - padded[:-2, 1:-1, 1:-1])
    flux = flux + face_y[:, 1:] * (centre - padded[1:-1, 2:, 1:-1]) + face_y[:, :-1] * (centre - padded[1:-1, :-2, 1:-1])
    flux = flux + face_z[:, :, 1:] * (centre - padded[1:-1, 1:-1, 2:]) + face_z[:, :, :-1] * (centre - padded[1:-1, 1:-1, :-2])
    return scale * flux


def sweep(field, source, level, scale, widen):
    return field + RELAX * (source - apply_operator(widen(field), level, scale)) / level[3]


def restrict_sum(field):
    depth, rows, cols = field.shape
    return field.reshape(depth // 2, 2, rows // 2, 2, cols // 2, 2).sum(axis=(1, 3, 5))


def coarsen_mean(field):
    return restrict_sum(field) * 0.125


def expand(coarse):
    depth, rows, cols = coarse.shape
    grown = jnp.broadcast_to(coarse[:, None, :, None, :, None], (depth, 2, rows, 2, cols, 2))
    return grown.reshape(depth * 2, rows * 2, cols * 2)


def coarse_solve(source, conduct, widen):
    level = level_setup(conduct, 4.0, widen)
    field = RELAX * source / level[3]
    for step_index in range(3):
        field = sweep(field, source, level, 4.0, widen)

    def turn(turn_index, current):
        for repeat in range(4):
            current = sweep(current, source, level, 4.0, widen)
        return current

    return lax.fori_loop(0, ITERS_C // 4 - 1, turn, field)


def reference(divergence, inverse_density):
    widen = widen_global
    fine = level_setup(inverse_density, 1.0, widen)
    pressure = RELAX * divergence / fine[3]
    pressure = sweep(pressure, divergence, fine, 1.0, widen)
    residue = divergence - apply_operator(widen(pressure), fine, 1.0)
    source_mid = restrict_sum(residue)
    density_mid = coarsen_mean(inverse_density)
    middle = level_setup(density_mid, 2.0, widen)
    correct_mid = RELAX * source_mid / middle[3]
    correct_mid = sweep(correct_mid, source_mid, middle, 2.0, widen)
    residue_mid = source_mid - apply_operator(widen(correct_mid), middle, 2.0)
    source_low = restrict_sum(residue_mid)
    density_low = coarsen_mean(density_mid)
    correction = coarse_solve(source_low, density_low, widen)
    correct_mid = correct_mid + expand(correction)
    correct_mid = sweep(correct_mid, source_mid, middle, 2.0, widen)
    correct_mid = sweep(correct_mid, source_mid, middle, 2.0, widen)
    pressure = pressure + expand(correct_mid)
    pressure = sweep(pressure, divergence, fine, 1.0, widen)
    pressure = sweep(pressure, divergence, fine, 1.0, widen)
    residual = divergence - apply_operator(widen(pressure), fine, 1.0)
    return pressure, residual
```

```python
import functools

import jax
import jax.numpy as jnp
from jax import lax
from jax.experimental import pallas as pl
from jax.experimental.pallas import tpu as pltpu
from jax.sharding import PartitionSpec as P

ITERS_C = 64
RELAX = 0.8
KEEP = 1.0 - RELAX
HF = 3
HM = 4
PAD = 8
Q = 4
A = Q // 2
MC = HM - 1
DIRS = [(dx, dy) for dx in (-1, 0, 1) for dy in (-1, 0, 1) if (dx, dy) != (0, 0)]
HI = lax.Precision.HIGHEST
F32 = jnp.float32


def dot(a, b):
    return jnp.dot(a, b, precision=HI, preferred_element_type=F32)


def select_matrix(rows, cols, test):
    r = lax.broadcasted_iota(jnp.int32, (rows, cols), 0)
    c = lax.broadcasted_iota(jnp.int32, (rows, cols), 1)
    return jnp.where(test(r, c), 1.0, 0.0).astype(F32)


def kernel(S, C, b_hbm, k_hbm, p_out, r_out,
           K, B, U, V, W, DD, UE, K1, B1, U1, V1, W1, D1, UE1,
           stage, GK, GB, KP, va, vb, wts, t256, t128,
           corner_out, corner_in, mid_out, mid_in, FF, F1,
           load_sem, send_f, recv_f, send_m, recv_m, send_g, recv_g, send_c, recv_c, send_k, recv_k, known):
    depth, rows, cols = b_hbm.shape
    FY = rows + 2 * PAD
    mdepth, mrows, mcols = depth // 2, rows // 2, cols // 2
    MY = mrows + 2 * PAD
    crows = mrows // 2
    CR = crows * C
    zw = mcols // Q
    XI = 2 * S // Q
    NV = XI * A
    s = lax.axis_index("span")
    c = lax.axis_index("cross")

    loads = [
        pltpu.make_async_copy(k_hbm, K.at[pl.ds(HF, depth), pl.ds(PAD, rows), :], load_sem.at[0]),
        pltpu.make_async_copy(b_hbm, B.at[pl.ds(HF, depth), pl.ds(PAD, rows), :], load_sem.at[1]),
    ]
    for x in loads:
        x.start()

    peers = [(i, j) for i in range(S) for j in range(C) if (i, j) != (0, 0)]

    def peer(o):
        return (lax.rem(s + o[0], S), lax.rem(c + o[1], C))


    def exists(dx, dy):
        return (s + dx >= 0) & (s + dx < S) & (c + dy >= 0) & (c + dy < C)

    def greet(sem, step):
        for dx, dy in DIRS:
            @pl.when(exists(dx * step, dy * step))
            def _(dx=dx, dy=dy):
                pl.semaphore_signal(
                    sem, inc=1, device_id=(s + dx * step, c + dy * step), device_id_type=pl.DeviceIdType.MESH
                )

    def heard(sem, step):
        present = [jnp.where(exists(dx * step, dy * step), 1, 0) for dx, dy in DIRS]
        pl.semaphore_wait(sem, sum(present))

    barrier = pltpu.get_barrier_semaphore()
    greet(barrier, 1)

    def spans(dx, dy, halo, h0, h1, n, r):
        if dx == 0:
            sl, dl, ln = halo, halo, n
        elif dx == 1:
            sl, dl, ln = halo + n - h1, halo - h1, h1 - h0
        else:
            sl, dl, ln = halo + h0, halo + n + h0, h1 - h0
        if dy == 0:
            sr, dr, rn = PAD, PAD, r
        elif dy == 1:
            sr, dr, rn = PAD + r - PAD, 0, PAD
        else:
            sr, dr, rn = PAD, PAD + r, PAD
        return sl, dl, ln, sr, dr, rn

    class Exchange:
        def __init__(self, buf, halo, h0, h1, n, r, ssem, rsem, slot, source=None, corners=True, along=False):
            self.items = []
            for q, (dx, dy) in enumerate(DIRS):
                if (dx == 0 and h0 > 0 and not along) or (dx != 0 and dy != 0 and not corners):
                    continue
                sl, dl, ln, sr, dr, rn = spans(dx, dy, halo, h0, h1, n, r)
                if source is None:
                    src = buf.at[pl.ds(sl, ln), pl.ds(sr, rn), :]
                else:
                    src = source.at[pl.ds(sl - halo, ln), pl.ds(sr - PAD, rn), :]
                copy = pltpu.make_async_remote_copy(
                    src_ref=src,
                    dst_ref=buf.at[pl.ds(dl, ln), pl.ds(dr, rn), :],
                    send_sem=ssem.at[slot, q],
                    recv_sem=rsem.at[slot, q],
                    device_id=(jnp.clip(s + dx, 0, S - 1), jnp.clip(c + dy, 0, C - 1)),
                    device_id_type=pl.DeviceIdType.MESH,
                )
                self.items.append((dx, dy, copy))

        def start(self):
            for dx, dy, copy in self.items:
                @pl.when(exists(dx, dy))
                def _(copy=copy):
                    copy.start()

        def wait_recv(self, span=None):
            for dx, dy, copy in self.items:
                if span is not None and span != abs(dx):
                    continue

                @pl.when(exists(-dx, -dy))
                def _(copy=copy):
                    copy.wait_recv()

        def wait_send(self):
            for dx, dy, copy in self.items:
                @pl.when(exists(dx, dy))
                def _(copy=copy):
                    copy.wait_send()

    def zero_edges(buf, halo, n, r):
        total = buf.shape[1]
        width = buf.shape[2]

        @pl.when(s == 0)
        def _():
            buf[0:halo] = jnp.zeros((halo, total, width), F32)

        @pl.when(s == S - 1)
        def _():
            buf[halo + n:] = jnp.zeros((halo, total, width), F32)

        @pl.when(c == 0)
        def _():
            buf[:, 0:PAD, :] = jnp.zeros((n + 2 * halo, PAD, width), F32)

        @pl.when(c == C - 1)
        def _():
            buf[:, PAD + r:, :] = jnp.zeros((n + 2 * halo, PAD, width), F32)

    class Corners:
        def __init__(self, slot, bufs):
            self.slot, self.bufs, self.items = slot, bufs, []
            for q, (dx, dy) in enumerate((i, j) for i in (-1, 1) for j in (-1, 1)):
                copy = pltpu.make_async_remote_copy(
                    src_ref=corner_out.at[slot, q],
                    dst_ref=corner_in.at[slot, q],
                    send_sem=send_c.at[slot, q],
                    recv_sem=recv_c.at[slot, q],
                    device_id=(jnp.clip(s + dx, 0, S - 1), jnp.clip(c + dy, 0, C - 1)),
                    device_id_type=pl.DeviceIdType.MESH,
                )
                self.items.append((q, dx, dy, copy))

        def pack(self):
            for q, dx, dy, copy in self.items:
                at = 0
                for buf in self.bufs:
                    for e in range(2):
                        layer = HF + depth - 1 - e if dx == 1 else HF + e
                        row = PAD + rows - 2 if dy == 1 else PAD
                        corner_out[self.slot, q, at:at + 2, :] = buf[layer, row:row + 2, :]
                        at += 2

        def start(self):
            for q, dx, dy, copy in self.items:
                @pl.when(exists(dx, dy))
                def _(copy=copy):
                    copy.start()

        def receive(self):
            for q, dx, dy, copy in self.items:
                @pl.when(exists(-dx, -dy))
                def _(q=q, dx=dx, dy=dy, copy=copy):
                    copy.wait_recv()
                    at = 0
                    for buf in self.bufs:
                        for e in range(2):
                            layer = HF - 1 - e if dx == 1 else HF + depth + e
                            row = PAD - 2 if dy == 1 else PAD + rows
                            buf[layer, row:row + 2, :] = corner_in[self.slot, q, at:at + 2, :]
                            at += 2

        def wait_send(self):
            for q, dx, dy, copy in self.items:
                @pl.when(exists(dx, dy))
                def _(copy=copy):
                    copy.wait_send()

    class MidCorners:
        def __init__(self, slot, buf):
            self.slot, self.buf, self.items = slot, buf, []
            for q, (dx, dy) in enumerate((i, j) for i in (-1, 1) for j in (-1, 1)):
                copy = pltpu.make_async_remote_copy(
                    src_ref=mid_out.at[slot, q],
                    dst_ref=mid_in.at[slot, q],
                    send_sem=send_k.at[slot, q],
                    recv_sem=recv_k.at[slot, q],
                    device_id=(jnp.clip(s + dx, 0, S - 1), jnp.clip(c + dy, 0, C - 1)),
                    device_id_type=pl.DeviceIdType.MESH,
                )
                self.items.append((q, dx, dy, copy))

        def pack(self):
            for q, dx, dy, copy in self.items:
                at = 0
                for e in range(1, MC + 1):
                    n = MC + 1 - e
                    layer = HM + mdepth - e if dx == 1 else HM + e - 1
                    row = PAD + mrows - n if dy == 1 else PAD
                    mid_out[self.slot, q, at:at + n, :] = self.buf[layer, row:row + n, :]
                    at += n

        def start(self):
            for q, dx, dy, copy in self.items:
                @pl.when(exists(dx, dy))
                def _(copy=copy):
                    copy.start()

        def receive(self):
            for q, dx, dy, copy in self.items:
                @pl.when(exists(-dx, -dy))
                def _(q=q, dx=dx, dy=dy, copy=copy):
                    copy.wait_recv()
                    at = 0
                    for e in range(1, MC + 1):
                        n = MC + 1 - e
                        layer = HM - e if dx == 1 else HM + mdepth + e - 1
                        row = PAD - n if dy == 1 else PAD + mrows
                        self.buf[layer, row:row + n, :] = mid_in[self.slot, q, at:at + n, :]
                        at += n

        def wait_send(self):
            for q, dx, dy, copy in self.items:
                @pl.when(exists(dx, dy))
                def _(copy=copy):
                    copy.wait_send()

    heard(barrier, 1)
    steps = []
    while 2 ** len(steps) < max(S, C) - 1:
        steps.append(2 ** len(steps))
    pending = list(enumerate(steps))

    def meet(rounds):
        for _ in range(min(rounds, len(pending))):
            turn, step = pending.pop(0)
            heard(known.at[turn], step)
            if pending:
                greet(known.at[pending[0][0]], pending[0][1])

    greet(known.at[0], steps[0])
    ek = Exchange(K, HF, 0, 3, depth, rows, send_f, recv_f, 0, k_hbm, corners=False)
    eb = Exchange(B, HF, 0, 2, depth, rows, send_f, recv_f, 1, b_hbm, corners=False)
    ek.start()
    eb.start()
    corner_out[...] = jnp.zeros(corner_out.shape, F32)
    for x in loads:
        x.wait()
    ec = Corners(0, (K, B))
    ec.pack()
    ec.start()

    for buf in (K, B, UE):
        for i in (0, HF + depth):
            for j in (0, PAD + rows):
                buf[i:i + HF, j:j + PAD, :] = jnp.zeros((HF, PAD, cols), F32)
        zero_edges(buf, HF, depth, rows)
    mid_out[...] = jnp.zeros(mid_out.shape, F32)
    for buf, value in ((K1, 1.0), (B1, 0.0), (UE1, 0.0)):
        for i in (0, HM + mdepth):
            for j in (0, PAD + mrows):
                buf[i:i + HM, j:j + PAD, :] = jnp.full((HM, PAD, mcols), value, F32)
        zero_edges(buf, HM, mdepth, mrows)
    KP[...] = jnp.zeros(KP.shape, F32)
    va[...] = jnp.zeros(va.shape, F32)
    vb[...] = jnp.zeros(vb.shape, F32)

    pair_z = select_matrix(cols, mcols, lambda r, q: (r == 2 * q) | (r == 2 * q + 1))
    def cell(q):
        return (q % zw) * A + (q // zw) % A

    low = [
        select_matrix(mcols, mcols, lambda r, q, p=p: (r // 2 == cell(q)) & (q // (A * zw) == p))
        for p in range(2)
    ]

    def restrict_rows(n):
        return t128[pl.ds(0, n, stride=2), :] + t128[pl.ds(1, n, stride=2), :]

    def to_low(mid):
        n = (mdepth // 2) * mrows
        for j in range(mdepth // 2):
            t128[j * mrows:(j + 1) * mrows, :] = mid(2 * j) + mid(2 * j + 1)
        packed = restrict_rows(n // 2)
        return dot(packed[0:crows], low[0]) + dot(packed[crows:2 * crows], low[1])

    for j in range(mdepth):
        t256[j * rows:(j + 1) * rows, :] = (
            K[HF + 2 * j, pl.ds(PAD, rows), :] + K[HF + 2 * j + 1, pl.ds(PAD, rows), :]
        )
    t128[...] = dot(t256[...], pair_z)
    K1[HM:HM + mdepth, PAD:PAD + mrows, :] = (0.125 * restrict_rows(mdepth * mrows)).reshape(mdepth, mrows, mcols)
    ek1 = Exchange(K1, HM, 0, HM, mdepth, mrows, send_m, recv_m, 0, corners=False)
    ek1c = MidCorners(0, K1)
    ek1c.pack()

    def gather(slot, dst):
        row = pl.multiple_of(c * crows, crows)
        return [
            pltpu.make_async_remote_copy(
                src_ref=stage.at[slot],
                dst_ref=dst.at[s, pl.ds(row, crows), :],
                send_sem=send_g.at[slot, n],
                recv_sem=recv_g.at[slot, n],
                device_id=peer(o),
                device_id_type=pl.DeviceIdType.MESH,
            )
            for n, o in reversed(list(enumerate(peers)))
        ]

    def own_block(dst, value):
        dst[s, pl.ds(pl.multiple_of(c * crows, crows), crows), :] = value

    k2 = 0.125 * to_low(lambda j: K1[HM + j, pl.ds(PAD, mrows), :])
    stage[0] = k2
    gk = gather(0, GK)
    own_block(GK, k2)

    def coupling(Kr, Fr, Vr, i):
        k0, v0 = Kr[i], Vr[i]
        n, m = v0.shape
        x = (k0 + Kr[i - 1]) * Vr[i - 1] + (k0 + Kr[i + 1]) * Vr[i + 1]
        y = Fr[0, i] * pltpu.roll(v0, 1, 0) + Fr[1, i] * pltpu.roll(v0, n - 1, 0)
        z = Fr[2, i] * pltpu.roll(v0, 1, 1) + Fr[3, i] * pltpu.roll(v0, m - 1, 1)
        return x + (y + z)

    def diagonal(Kr, Fr, i, factor, halo, n, r):
        k0 = Kr[i]
        height, m = k0.shape
        lane = lax.broadcasted_iota(jnp.int32, k0.shape, 1)
        y0, y1 = pltpu.roll(k0, 1, 0), pltpu.roll(k0, height - 1, 0)
        z0 = jnp.where(lane == 0, 0.0, pltpu.roll(k0, 1, 1))
        z1 = jnp.where(lane == m - 1, 0.0, pltpu.roll(k0, m - 1, 1))
        Fr[0, i] = k0 + y0
        Fr[1, i] = k0 + y1
        Fr[2, i] = jnp.where(lane == 0, 0.0, k0 + z0)
        Fr[3, i] = jnp.where(lane == m - 1, 0.0, k0 + z1)
        total = factor * (6.0 * k0 + ((Kr[i - 1] + Kr[i + 1]) + ((y0 + y1) + (z0 + z1))))
        y = lax.broadcasted_iota(jnp.int32, k0.shape, 0) + (c * r - PAD)
        inside = (y >= 0) & (y < r * C)
        x = s * n - halo + i
        xin = jnp.where((x >= 0) & (x < n * S), 1.0, 0.0).astype(F32)
        total = jnp.where(inside, total, 1.0) + (1.0 - xin)
        return total, jnp.where(inside, RELAX / total, 0.0) * xin

    def sweep(Kr, Fr, Br, Wr, src, dst, factor, layers):
        for i in layers:
            dst[i] = KEEP * src[i] + Wr[i] * (Br[i] + factor * coupling(Kr, Fr, src, i))

    def split(lo, hi, inner_lo, inner_hi):
        return list(range(inner_lo, inner_hi)), [i for i in range(lo, hi) if not inner_lo <= i < inner_hi]

    def fine_start(layers):
        for i in layers:
            total, inv = diagonal(K, FF, i, 0.5, HF, depth, rows)
            DD[i] = total
            W[i] = inv
            U[i] = B[i] * inv

    own = pl.ds(PAD, rows)

    def fine_residual(i):
        return B[i] - DD[i] * V[i] + 0.5 * coupling(K, FF, V, i)

    def fine_pairs(pairs):
        for j in pairs:
            i = HF + 2 * j
            both = fine_residual(i) + fine_residual(i + 1)
            t256[j * rows:(j + 1) * rows, :] = both[PAD:PAD + rows]

    end = HF + depth
    in_d, out_d = split(HF - 2, end + 2, HF + 1, end - 1)
    in_u, out_u = split(HF - 1, end + 1, HF + 2, end - 2)
    in_r, out_r = split(0, mdepth, 2, mdepth - 2)
    meet(1)
    ek.wait_recv(0)
    eb.wait_recv(0)
    fine_start(in_d)
    sweep(K, FF, B, W, U, V, 0.5, in_u)
    fine_pairs(in_r)
    meet(len(steps))
    ek.wait_recv(1)
    eb.wait_recv(1)
    ec.receive()
    ek1.start()
    ek1c.start()
    for x in gk:
        x.start()
    fine_start(out_d)
    sweep(K, FF, B, W, U, V, 0.5, out_u)
    fine_pairs(out_r)

    t128[...] = dot(t256[...], pair_z)
    B1[HM:HM + mdepth, PAD:PAD + mrows, :] = restrict_rows(mdepth * mrows).reshape(mdepth, mrows, mcols)
    eb1 = Exchange(B1, HM, 0, MC, mdepth, mrows, send_m, recv_m, 1, corners=False)
    eb1.start()
    eb1c = MidCorners(1, B1)
    eb1c.pack()
    eb1c.start()

    UE[HF - 1:HF + depth + 1, PAD:PAD + rows, :] = V[HF - 1:HF + depth + 1, PAD:PAD + rows, :]
    ek1.wait_recv()
    ek1c.receive()

    for i in range(HM - 3, HM + mdepth + 3):
        total, inv = diagonal(K1, F1, i, 1.0, HM, mdepth, mrows)
        D1[i] = total
        W1[i] = inv

    for x in gk:
        x.wait_recv()
    inner = pl.ds(PAD, CR)
    lane = lax.broadcasted_iota(jnp.int32, (CR, mcols), 1)
    block = lane // zw
    z_lo = lane % zw == 0
    z_hi = lane % zw == zw - 1

    def arrange(src, x, a):
        group = (x % 2) * A + a
        out = None
        for q in range(Q):
            v = src[q * (S // Q) + x // 2]
            if q != group:
                v = pltpu.roll(v, ((q - group) * zw) % mcols, 1)
            out = v if out is None else jnp.where(block == q, v, out)
        return out

    def neighbours(ref, x, a, fields):
        before, here, after = fields
        i = x * A + a
        return (
            before[a],
            after[a],
            ref[i, pl.ds(PAD - 1, CR), :],
            ref[i, pl.ds(PAD + 1, CR), :],
            here[a - 1] if a > 0 else pltpu.roll(here[A - 1], 1, 1),
            here[a + 1] if a < A - 1 else pltpu.roll(here[0], mcols - 1, 1),
        )

    def layer(ref, x):
        return [ref[x * A + a, inner, :] for a in range(A)]

    def columns(ref):
        first, last = layer(ref, 0), layer(ref, XI - 1)
        before = [pltpu.roll(v, zw, 1) for v in last]
        wrap = [pltpu.roll(v, mcols - zw, 1) for v in first]
        here = first
        for x in range(XI):
            after = (last if x + 1 == XI - 1 else layer(ref, x + 1)) if x < XI - 1 else wrap
            yield x, (before, here, after)
            before, here = here, after

    for x in range(XI):
        for a in range(A):
            KP[x * A + a, inner, :] = arrange(GK, x, a)
    for x, fields in columns(KP):
        for a in range(A):
            k0 = fields[1][a]
            near = list(neighbours(KP, x, a, fields))
            outside = {}
            if x == 0:
                outside[0] = block == 0
            if x == XI - 1:
                outside[1] = block == Q - 1
            if a == 0:
                outside[4] = z_lo
            if a == A - 1:
                outside[5] = z_hi
            for q, mask in outside.items():
                near[q] = jnp.where(mask, 0.0, near[q])
            total = 2.0 * (6.0 * k0 + (((near[0] + near[1]) + (near[2] + near[3])) + (near[4] + near[5])))
            inv = RELAX / total
            for q in range(6):
                w = 2.0 * (k0 + near[q]) * inv
                if q in outside:
                    w = jnp.where(outside[q], 0.0, w)
                wts[q, x * A + a] = w
            wts[6, x * A + a] = inv

    eb1.wait_recv()
    eb1c.receive()
    for i in range(HM - 2, HM + mdepth + 2):
        U1[i] = W1[i] * B1[i]
    sweep(K1, F1, B1, W1, U1, V1, 1.0, range(HM - 1, HM + mdepth + 1))

    def mid_residual(j):
        i = HM + j
        return (B1[i] - D1[i] * V1[i] + coupling(K1, F1, V1, i))[PAD:PAD + mrows]

    b2 = to_low(mid_residual)
    stage[1] = b2
    gb = gather(1, GB)
    for x in gb:
        x.start()
    own_block(GB, b2)

    UE1[HM - 1:HM + mdepth + 1, PAD:PAD + mrows, :] = V1[HM - 1:HM + mdepth + 1, PAD:PAD + mrows, :]
    eu1 = Exchange(UE1, HM, 1, HM, mdepth, mrows, send_m, recv_m, 2, corners=False, along=True)
    eu1c = MidCorners(2, UE1)
    eu1c.pack()
    eu = Exchange(UE, HF, 1, HF, depth, rows, send_f, recv_f, 2, corners=False, along=True)
    euc = Corners(1, (UE,))
    euc.pack()

    for x in gb:
        x.wait_recv()
    eu1.start()
    eu1c.start()
    eu.start()
    euc.start()
    for x in range(XI):
        for a in range(A):
            i = x * A + a
            const = wts[6, i] * arrange(GB, x, a)
            wts[6, i] = const
            va[i, inner, :] = const

    def coarse_sweep(src, dst):
        for x, fields in columns(src):
            for a in range(A):
                i = x * A + a
                near = neighbours(src, x, a, fields)
                acc = [wts[q, i] * near[q] for q in range(6)]
                dst[i, inner, :] = (
                    ((acc[0] + acc[1]) + (acc[2] + acc[3]))
                    + ((acc[4] + acc[5]) + (KEEP * fields[1][a] + wts[6, i]))
                )

    @pl.loop(0, (ITERS_C - 1) // 2)
    def _(t):
        coarse_sweep(va, vb)
        coarse_sweep(vb, va)

    coarse_sweep(va, vb)

    eu1.wait_recv()
    eu1c.receive()
    grow_low = [
        select_matrix(mcols, mcols, lambda r, q, p=p: (q // 2 == cell(r)) & (r // (A * zw) == p))
        for p in range(2)
    ]
    window = crows + 2 * PAD
    rows_low = select_matrix(MY, window, lambda r, q: (r == 2 * (q - PAD // 2)) | (r == 2 * (q - PAD // 2) + 1))
    wide_block = lax.broadcasted_iota(jnp.int32, (window, mcols), 1) // zw

    def own_pair(n):
        t = s + n - 1
        at = lax.rem(t + S, S)
        q = at // (S // Q)
        x = 2 * lax.rem(at, S // Q)
        out = jnp.zeros((window, mcols), F32)
        for e in range(2):
            for a in range(A):
                group = e * A + a
                v = vb[(x + e) * A + a, pl.ds(pl.multiple_of(c * crows, crows), window), :]
                v = pltpu.roll(v, lax.rem(group - q + Q, Q) * zw, 1)
                out = jnp.where((wide_block == group) & (t >= 0) & (t < S), v, out)
        return out

    tall = jnp.concatenate([dot(rows_low, own_pair(n)) for n in range(3)], axis=0)
    for p in range(2):
        grown = dot(tall, grow_low[p])
        for n in range(3):
            for e in range(2):
                i = 4 * n + 2 * p + e
                U1[i] = UE1[i] + grown[n * MY:(n + 1) * MY]
    sweep(K1, F1, B1, W1, U1, V1, 1.0, range(HM - 3, HM + mdepth + 3))
    sweep(K1, F1, B1, W1, V1, U1, 1.0, range(HM - 2, HM + mdepth + 2))

    eu.wait_recv()
    euc.receive()
    grow_z = select_matrix(mcols, cols, lambda r, q: (q == 2 * r) | (q == 2 * r + 1))
    rows_mid = select_matrix(FY, MY, lambda r, q: (r == 2 * (q - PAD // 2)) | (r == 2 * (q - PAD // 2) + 1))
    mids = range(HM - 2, HM + mdepth + 2)
    all_grown = dot(jnp.concatenate([dot(rows_mid, U1[m]) for m in mids], axis=0), grow_z)
    for q, m in enumerate(mids):
        grown = all_grown[q * FY:(q + 1) * FY]
        for i in (2 * (m - HM) + HF, 2 * (m - HM) + HF + 1):
            if 0 <= i < depth + 2 * HF:
                V[i] = UE[i] + grown
    sweep(K, FF, B, W, V, U, 0.5, range(HF - 2, HF + depth + 2))
    sweep(K, FF, B, W, U, V, 0.5, range(HF - 1, HF + depth + 1))

    for j in range(depth):
        i = HF + j
        p_out[j] = V[i, own, :]
        r_out[j] = fine_residual(i)[PAD:PAD + rows]

    for e in (ek, eb, ec, ek1, ek1c, eb1, eb1c, eu1, eu1c, eu, euc):
        e.wait_send()
    for x in gk + gb:
        x.wait_send()


def hand_over(p_in, r_in, p_out, r_out, sems):
    copies = [
        pltpu.make_async_copy(p_in, p_out, sems.at[0]),
        pltpu.make_async_copy(r_in, r_out, sems.at[1]),
    ]
    for x in copies:
        x.start()
    for x in copies:
        x.wait()


def local(S, C, divergence, inverse_density):
    depth, rows, cols = divergence.shape
    mdepth, mrows, mcols = depth // 2, rows // 2, cols // 2
    crows = mrows // 2
    fine = pltpu.VMEM((depth + 2 * HF, rows + 2 * PAD, cols), F32)
    mid = pltpu.VMEM((mdepth + 2 * HM, mrows + 2 * PAD, mcols), F32)
    low = pltpu.VMEM((S, crows * C, mcols), F32)
    wide = pltpu.VMEM((S, crows * C + 2 * PAD, mcols), F32)
    n = len(DIRS)
    peers = S * C - 1
    dma = pltpu.SemaphoreType.DMA
    out = jax.ShapeDtypeStruct(divergence.shape, F32)
    inner = pl.pallas_call(
        functools.partial(kernel, S, C),
        out_shape=(out, out),
        in_specs=[pl.BlockSpec(memory_space=pl.ANY)] * 2,
        out_specs=(pl.BlockSpec(memory_space=pltpu.VMEM),) * 2,
        scratch_shapes=[fine] * 7 + [mid] * 7 + [
            pltpu.VMEM((2, crows, mcols), F32), low, low, wide, wide, wide,
            pltpu.VMEM((7, S, crows * C, mcols), F32),
            pltpu.VMEM((mdepth * rows, cols), F32),
            pltpu.VMEM((mdepth * rows, mcols), F32),
            pltpu.VMEM((2, 4, 8, cols), F32), pltpu.VMEM((2, 4, 8, cols), F32),
            pltpu.VMEM((3, 4, 8, mcols), F32), pltpu.VMEM((3, 4, 8, mcols), F32),
            pltpu.VMEM((4,) + fine.shape, F32), pltpu.VMEM((4,) + mid.shape, F32),
            dma((2,)), dma((3, n)), dma((3, n)), dma((3, n)), dma((3, n)),
            dma((2, peers)), dma((2, peers)), dma((2, 4)), dma((2, 4)), dma((3, 4)), dma((3, 4)),
            pltpu.SemaphoreType.REGULAR((max(S, C).bit_length(),)),
        ],
        compiler_params=pltpu.CompilerParams(collective_id=0, has_side_effects=True),
    )(divergence, inverse_density)
    return pl.pallas_call(
        hand_over,
        out_shape=(out, out),
        in_specs=[pl.BlockSpec(memory_space=pltpu.VMEM)] * 2,
        out_specs=(pl.BlockSpec(memory_space=pl.ANY),) * 2,
        scratch_shapes=[dma((2,))],
    )(*inner)


def solution(mesh):
    placed = P("span", "cross", None)
    return jax.shard_map(
        functools.partial(local, mesh.shape["span"], mesh.shape["cross"]),
        mesh=mesh,
        in_specs=(placed, placed),
        out_specs=(placed, placed),
        check_vma=False,
    )
```

```python
import functools

import jax
import jax.numpy as jnp
from jax import lax
from jax.experimental import pallas as pl
from jax.experimental.pallas import tpu as pltpu
from jax.sharding import PartitionSpec as P

ITERS_C = 64
RELAX = 0.8
KEEP = 1.0 - RELAX
HF = 3
HM = 4
PAD = 8
Q = 4
A = Q // 2
MC = HM - 1
DIRS = [(dx, dy) for dx in (-1, 0, 1) for dy in (-1, 0, 1) if (dx, dy) != (0, 0)]
HI = lax.Precision.HIGHEST
F32 = jnp.float32


def dot(a, b):
    return jnp.dot(a, b, precision=HI, preferred_element_type=F32)


def select_matrix(rows, cols, test):
    r = lax.broadcasted_iota(jnp.int32, (rows, cols), 0)
    c = lax.broadcasted_iota(jnp.int32, (rows, cols), 1)
    return jnp.where(test(r, c), 1.0, 0.0).astype(F32)


def kernel(S, C, b_hbm, k_hbm, p_out, r_out,
           K, B, U, V, W, DD, UE, K1, B1, U1, V1, W1, D1, UE1,
           stage, GK, GB, KP, va, vb, wts, t256, t128,
           corner_out, corner_in, mid_out, mid_in, FF, F1,
           load_sem, send_f, recv_f, send_m, recv_m, send_g, recv_g, send_c, recv_c, send_k, recv_k, known):
    depth, rows, cols = b_hbm.shape
    FY = rows + 2 * PAD
    mdepth, mrows, mcols = depth // 2, rows // 2, cols // 2
    MY = mrows + 2 * PAD
    crows = mrows // 2
    CR = crows * C
    zw = mcols // Q
    XI = 2 * S // Q
    NV = XI * A
    s = lax.axis_index("span")
    c = lax.axis_index("cross")

    loads = [
        pltpu.make_async_copy(k_hbm, K.at[pl.ds(HF, depth), pl.ds(PAD, rows), :], load_sem.at[0]),
        pltpu.make_async_copy(b_hbm, B.at[pl.ds(HF, depth), pl.ds(PAD, rows), :], load_sem.at[1]),
    ]
    for x in loads:
        x.start()

    peers = [(i, j) for i in range(S) for j in range(C) if (i, j) != (0, 0)]

    def peer(o):
        return (lax.rem(s + o[0], S), lax.rem(c + o[1], C))


    def exists(dx, dy):
        return (s + dx >= 0) & (s + dx < S) & (c + dy >= 0) & (c + dy < C)

    def greet(sem, step):
        for dx, dy in DIRS:
            @pl.when(exists(dx * step, dy * step))
            def _(dx=dx, dy=dy):
                pl.semaphore_signal(
                    sem, inc=1, device_id=(s + dx * step, c + dy * step), device_id_type=pl.DeviceIdType.MESH
                )

    def heard(sem, step):
        present = [jnp.where(exists(dx * step, dy * step), 1, 0) for dx, dy in DIRS]
        pl.semaphore_wait(sem, sum(present))

    barrier = pltpu.get_barrier_semaphore()
    greet(barrier, 1)

    def spans(dx, dy, halo, h0, h1, n, r):
        if dx == 0:
            sl, dl, ln = halo, halo, n
        elif dx == 1:
            sl, dl, ln = halo + n - h1, halo - h1, h1 - h0
        else:
            sl, dl, ln = halo + h0, halo + n + h0, h1 - h0
        if dy == 0:
            sr, dr, rn = PAD, PAD, r
        elif dy == 1:
            sr, dr, rn = PAD + r - PAD, 0, PAD
        else:
            sr, dr, rn = PAD, PAD + r, PAD
        return sl, dl, ln, sr, dr, rn

    class Exchange:
        def __init__(self, buf, halo, h0, h1, n, r, ssem, rsem, slot, source=None, corners=True, along=False):
            self.items = []
            for q, (dx, dy) in enumerate(DIRS):
                if (dx == 0 and h0 > 0 and not along) or (dx != 0 and dy != 0 and not corners):
                    continue
                sl, dl, ln, sr, dr, rn = spans(dx, dy, halo, h0, h1, n, r)
                if source is None:
                    src = buf.at[pl.ds(sl, ln), pl.ds(sr, rn), :]
                else:
                    src = source.at[pl.ds(sl - halo, ln), pl.ds(sr - PAD, rn), :]
                copy = pltpu.make_async_remote_copy(
                    src_ref=src,
                    dst_ref=buf.at[pl.ds(dl, ln), pl.ds(dr, rn), :],
                    send_sem=ssem.at[slot, q],
                    recv_sem=rsem.at[slot, q],
                    device_id=(jnp.clip(s + dx, 0, S - 1), jnp.clip(c + dy, 0, C - 1)),
                    device_id_type=pl.DeviceIdType.MESH,
                )
                self.items.append((dx, dy, copy))

        def start(self):
            for dx, dy, copy in self.items:
                @pl.when(exists(dx, dy))
                def _(copy=copy):
                    copy.start()

        def wait_recv(self, span=None):
            for dx, dy, copy in self.items:
                if span is not None and span != abs(dx):
                    continue

                @pl.when(exists(-dx, -dy))
                def _(copy=copy):
                    copy.wait_recv()

        def wait_send(self):
            for dx, dy, copy in self.items:
                @pl.when(exists(dx, dy))
                def _(copy=copy):
                    copy.wait_send()

    def zero_edges(buf, halo, n, r):
        total = buf.shape[1]
        width = buf.shape[2]

        @pl.when(s == 0)
        def _():
            buf[0:halo] = jnp.zeros((halo, total, width), F32)

        @pl.when(s == S - 1)
        def _():
            buf[halo + n:] = jnp.zeros((halo, total, width), F32)

        @pl.when(c == 0)
        def _():
            buf[:, 0:PAD, :] = jnp.zeros((n + 2 * halo, PAD, width), F32)

        @pl.when(c == C - 1)
        def _():
            buf[:, PAD + r:, :] = jnp.zeros((n + 2 * halo, PAD, width), F32)

    class Corners:
        def __init__(self, slot, bufs):
            self.slot, self.bufs, self.items = slot, bufs, []
            for q, (dx, dy) in enumerate((i, j) for i in (-1, 1) for j in (-1, 1)):
                copy = pltpu.make_async_remote_copy(
                    src_ref=corner_out.at[slot, q],
                    dst_ref=corner_in.at[slot, q],
                    send_sem=send_c.at[slot, q],
                    recv_sem=recv_c.at[slot, q],
                    device_id=(jnp.clip(s + dx, 0, S - 1), jnp.clip(c + dy, 0, C - 1)),
                    device_id_type=pl.DeviceIdType.MESH,
                )
                self.items.append((q, dx, dy, copy))

        def pack(self):
            for q, dx, dy, copy in self.items:
                at = 0
                for buf in self.bufs:
                    for e in range(2):
                        layer = HF + depth - 1 - e if dx == 1 else HF + e
                        row = PAD + rows - 2 if dy == 1 else PAD
                        corner_out[self.slot, q, at:at + 2, :] = buf[layer, row:row + 2, :]
                        at += 2

        def start(self):
            for q, dx, dy, copy in self.items:
                @pl.when(exists(dx, dy))
                def _(copy=copy):
                    copy.start()

        def receive(self):
            for q, dx, dy, copy in self.items:
                @pl.when(exists(-dx, -dy))
                def _(q=q, dx=dx, dy=dy, copy=copy):
                    copy.wait_recv()
                    at = 0
                    for buf in self.bufs:
                        for e in range(2):
                            layer = HF - 1 - e if dx == 1 else HF + depth + e
                            row = PAD - 2 if dy == 1 else PAD + rows
                            buf[layer, row:row + 2, :] = corner_in[self.slot, q, at:at + 2, :]
                            at += 2

        def wait_send(self):
            for q, dx, dy, copy in self.items:
                @pl.when(exists(dx, dy))
                def _(copy=copy):
                    copy.wait_send()

    class MidCorners:
        def __init__(self, slot, buf):
            self.slot, self.buf, self.items = slot, buf, []
            for q, (dx, dy) in enumerate((i, j) for i in (-1, 1) for j in (-1, 1)):
                copy = pltpu.make_async_remote_copy(
                    src_ref=mid_out.at[slot, q],
                    dst_ref=mid_in.at[slot, q],
                    send_sem=send_k.at[slot, q],
                    recv_sem=recv_k.at[slot, q],
                    device_id=(jnp.clip(s + dx, 0, S - 1), jnp.clip(c + dy, 0, C - 1)),
                    device_id_type=pl.DeviceIdType.MESH,
                )
                self.items.append((q, dx, dy, copy))

        def pack(self):
            for q, dx, dy, copy in self.items:
                at = 0
                for e in range(1, MC + 1):
                    n = MC + 1 - e
                    layer = HM + mdepth - e if dx == 1 else HM + e - 1
                    row = PAD + mrows - n if dy == 1 else PAD
                    mid_out[self.slot, q, at:at + n, :] = self.buf[layer, row:row + n, :]
                    at += n

        def start(self):
            for q, dx, dy, copy in self.items:
                @pl.when(exists(dx, dy))
                def _(copy=copy):
                    copy.start()

        def receive(self):
            for q, dx, dy, copy in self.items:
                @pl.when(exists(-dx, -dy))
                def _(q=q, dx=dx, dy=dy, copy=copy):
                    copy.wait_recv()
                    at = 0
                    for e in range(1, MC + 1):
                        n = MC + 1 - e
                        layer = HM - e if dx == 1 else HM + mdepth + e - 1
                        row = PAD - n if dy == 1 else PAD + mrows
                        self.buf[layer, row:row + n, :] = mid_in[self.slot, q, at:at + n, :]
                        at += n

        def wait_send(self):
            for q, dx, dy, copy in self.items:
                @pl.when(exists(dx, dy))
                def _(copy=copy):
                    copy.wait_send()

    corner_out[...] = jnp.zeros(corner_out.shape, F32)
    for buf in (K, B, UE):
        for i in (0, HF + depth):
            for j in (0, PAD + rows):
                buf[i:i + HF, j:j + PAD, :] = jnp.zeros((HF, PAD, cols), F32)
        zero_edges(buf, HF, depth, rows)
    mid_out[...] = jnp.zeros(mid_out.shape, F32)
    for buf, value in ((K1, 1.0), (B1, 0.0), (UE1, 0.0)):
        for i in (0, HM + mdepth):
            for j in (0, PAD + mrows):
                buf[i:i + HM, j:j + PAD, :] = jnp.full((HM, PAD, mcols), value, F32)
        zero_edges(buf, HM, mdepth, mrows)
    KP[...] = jnp.zeros(KP.shape, F32)
    va[...] = jnp.zeros(va.shape, F32)
    vb[...] = jnp.zeros(vb.shape, F32)

    heard(barrier, 1)
    steps = []
    while 2 ** len(steps) < max(S, C) - 1:
        steps.append(2 ** len(steps))
    pending = list(enumerate(steps))

    def meet(rounds):
        for _ in range(min(rounds, len(pending))):
            turn, step = pending.pop(0)
            heard(known.at[turn], step)
            if pending:
                greet(known.at[pending[0][0]], pending[0][1])

    greet(known.at[0], steps[0])
    ek = Exchange(K, HF, 0, 3, depth, rows, send_f, recv_f, 0, k_hbm, corners=False)
    eb = Exchange(B, HF, 0, 2, depth, rows, send_f, recv_f, 1, b_hbm, corners=False)
    ek.start()
    eb.start()
    for x in loads:
        x.wait()
    ec = Corners(0, (K, B))
    ec.pack()
    ec.start()

    pair_z = select_matrix(cols, mcols, lambda r, q: (r == 2 * q) | (r == 2 * q + 1))
    def cell(q):
        return (q % zw) * A + (q // zw) % A

    low = [
        select_matrix(mcols, mcols, lambda r, q, p=p: (r // 2 == cell(q)) & (q // (A * zw) == p))
        for p in range(2)
    ]

    def restrict_rows(n):
        return t128[pl.ds(0, n, stride=2), :] + t128[pl.ds(1, n, stride=2), :]

    def to_low(mid):
        n = (mdepth // 2) * mrows
        for j in range(mdepth // 2):
            t128[j * mrows:(j + 1) * mrows, :] = mid(2 * j) + mid(2 * j + 1)
        packed = restrict_rows(n // 2)
        return dot(packed[0:crows], low[0]) + dot(packed[crows:2 * crows], low[1])

    for j in range(mdepth):
        t256[j * rows:(j + 1) * rows, :] = (
            K[HF + 2 * j, pl.ds(PAD, rows), :] + K[HF + 2 * j + 1, pl.ds(PAD, rows), :]
        )
    t128[...] = dot(t256[...], pair_z)
    K1[HM:HM + mdepth, PAD:PAD + mrows, :] = (0.125 * restrict_rows(mdepth * mrows)).reshape(mdepth, mrows, mcols)
    ek1 = Exchange(K1, HM, 0, HM, mdepth, mrows, send_m, recv_m, 0, corners=False)
    ek1c = MidCorners(0, K1)
    ek1c.pack()

    def gather(slot, dst):
        row = pl.multiple_of(c * crows, crows)
        return [
            pltpu.make_async_remote_copy(
                src_ref=stage.at[slot],
                dst_ref=dst.at[s, pl.ds(row, crows), :],
                send_sem=send_g.at[slot, n],
                recv_sem=recv_g.at[slot, n],
                device_id=peer(o),
                device_id_type=pl.DeviceIdType.MESH,
            )
            for n, o in reversed(list(enumerate(peers)))
        ]

    def own_block(dst, value):
        dst[s, pl.ds(pl.multiple_of(c * crows, crows), crows), :] = value

    k2 = 0.125 * to_low(lambda j: K1[HM + j, pl.ds(PAD, mrows), :])
    stage[0] = k2
    gk = gather(0, GK)
    own_block(GK, k2)

    def coupling(Kr, Fr, Vr, i):
        k0, v0 = Kr[i], Vr[i]
        n, m = v0.shape
        x = (k0 + Kr[i - 1]) * Vr[i - 1] + (k0 + Kr[i + 1]) * Vr[i + 1]
        y = Fr[0, i] * pltpu.roll(v0, 1, 0) + Fr[1, i] * pltpu.roll(v0, n - 1, 0)
        z = Fr[2, i] * pltpu.roll(v0, 1, 1) + Fr[3, i] * pltpu.roll(v0, m - 1, 1)
        return x + (y + z)

    def diagonal(Kr, Fr, i, factor, halo, n, r):
        k0 = Kr[i]
        height, m = k0.shape
        lane = lax.broadcasted_iota(jnp.int32, k0.shape, 1)
        y0, y1 = pltpu.roll(k0, 1, 0), pltpu.roll(k0, height - 1, 0)
        z0 = jnp.where(lane == 0, 0.0, pltpu.roll(k0, 1, 1))
        z1 = jnp.where(lane == m - 1, 0.0, pltpu.roll(k0, m - 1, 1))
        Fr[0, i] = k0 + y0
        Fr[1, i] = k0 + y1
        Fr[2, i] = jnp.where(lane == 0, 0.0, k0 + z0)
        Fr[3, i] = jnp.where(lane == m - 1, 0.0, k0 + z1)
        total = factor * (6.0 * k0 + ((Kr[i - 1] + Kr[i + 1]) + ((y0 + y1) + (z0 + z1))))
        y = lax.broadcasted_iota(jnp.int32, k0.shape, 0) + (c * r - PAD)
        inside = (y >= 0) & (y < r * C)
        x = s * n - halo + i
        xin = jnp.where((x >= 0) & (x < n * S), 1.0, 0.0).astype(F32)
        total = jnp.where(inside, total, 1.0) + (1.0 - xin)
        return total, jnp.where(inside, RELAX / total, 0.0) * xin

    def sweep(Kr, Fr, Br, Wr, src, dst, factor, layers):
        for i in layers:
            dst[i] = KEEP * src[i] + Wr[i] * (Br[i] + factor * coupling(Kr, Fr, src, i))

    def split(lo, hi, inner_lo, inner_hi):
        return list(range(inner_lo, inner_hi)), [i for i in range(lo, hi) if not inner_lo <= i < inner_hi]

    def fine_start(layers):
        for i in layers:
            total, inv = diagonal(K, FF, i, 0.5, HF, depth, rows)
            DD[i] = total
            W[i] = inv
            U[i] = B[i] * inv

    own = pl.ds(PAD, rows)

    def fine_residual(i):
        return B[i] - DD[i] * V[i] + 0.5 * coupling(K, FF, V, i)

    def fine_pairs(pairs):
        for j in pairs:
            i = HF + 2 * j
            both = fine_residual(i) + fine_residual(i + 1)
            t256[j * rows:(j + 1) * rows, :] = both[PAD:PAD + rows]

    end = HF + depth
    in_d, out_d = split(HF - 2, end + 2, HF + 1, end - 1)
    in_u, out_u = split(HF - 1, end + 1, HF + 2, end - 2)
    in_r, out_r = split(0, mdepth, 2, mdepth - 2)
    meet(1)
    ek.wait_recv(0)
    eb.wait_recv(0)
    fine_start(in_d)
    sweep(K, FF, B, W, U, V, 0.5, in_u)
    fine_pairs(in_r)
    ek.wait_recv(1)
    eb.wait_recv(1)
    ec.receive()
    ek1.start()
    ek1c.start()
    meet(1)
    fine_start(out_d)
    sweep(K, FF, B, W, U, V, 0.5, out_u)
    fine_pairs(out_r)

    t128[...] = dot(t256[...], pair_z)
    B1[HM:HM + mdepth, PAD:PAD + mrows, :] = restrict_rows(mdepth * mrows).reshape(mdepth, mrows, mcols)
    eb1 = Exchange(B1, HM, 0, MC, mdepth, mrows, send_m, recv_m, 1, corners=False)
    eb1.start()
    eb1c = MidCorners(1, B1)
    eb1c.pack()
    eb1c.start()
    meet(len(steps))
    for x in gk:
        x.start()

    UE[HF - 1:HF + depth + 1, PAD:PAD + rows, :] = V[HF - 1:HF + depth + 1, PAD:PAD + rows, :]
    ek1.wait_recv()
    ek1c.receive()

    for i in range(HM - 3, HM + mdepth + 3):
        total, inv = diagonal(K1, F1, i, 1.0, HM, mdepth, mrows)
        D1[i] = total
        W1[i] = inv

    eb1.wait_recv()
    eb1c.receive()
    for i in range(HM - 2, HM + mdepth + 2):
        U1[i] = W1[i] * B1[i]
    sweep(K1, F1, B1, W1, U1, V1, 1.0, range(HM - 1, HM + mdepth + 1))

    def mid_residual(j):
        i = HM + j
        return (B1[i] - D1[i] * V1[i] + coupling(K1, F1, V1, i))[PAD:PAD + mrows]

    b2 = to_low(mid_residual)
    stage[1] = b2
    gb = gather(1, GB)
    for x in gb:
        x.start()
    own_block(GB, b2)

    UE1[HM - 1:HM + mdepth + 1, PAD:PAD + mrows, :] = V1[HM - 1:HM + mdepth + 1, PAD:PAD + mrows, :]
    eu1 = Exchange(UE1, HM, 1, HM, mdepth, mrows, send_m, recv_m, 2, corners=False, along=True)
    eu1c = MidCorners(2, UE1)
    eu1c.pack()
    eu = Exchange(UE, HF, 1, HF, depth, rows, send_f, recv_f, 2, corners=False, along=True)
    euc = Corners(1, (UE,))
    euc.pack()

    for x in gk:
        x.wait_recv()
    inner = pl.ds(PAD, CR)
    lane = lax.broadcasted_iota(jnp.int32, (CR, mcols), 1)
    block = lane // zw
    z_lo = lane % zw == 0
    z_hi = lane % zw == zw - 1

    def arrange(src, x, a):
        group = (x % 2) * A + a
        out = None
        for q in range(Q):
            v = src[q * (S // Q) + x // 2]
            if q != group:
                v = pltpu.roll(v, ((q - group) * zw) % mcols, 1)
            out = v if out is None else jnp.where(block == q, v, out)
        return out

    def neighbours(ref, x, a, fields):
        before, here, after = fields
        i = x * A + a
        return (
            before[a],
            after[a],
            ref[i, pl.ds(PAD - 1, CR), :],
            ref[i, pl.ds(PAD + 1, CR), :],
            here[a - 1] if a > 0 else pltpu.roll(here[A - 1], 1, 1),
            here[a + 1] if a < A - 1 else pltpu.roll(here[0], mcols - 1, 1),
        )

    def layer(ref, x):
        return [ref[x * A + a, inner, :] for a in range(A)]

    def columns(ref):
        first, last = layer(ref, 0), layer(ref, XI - 1)
        before = [pltpu.roll(v, zw, 1) for v in last]
        wrap = [pltpu.roll(v, mcols - zw, 1) for v in first]
        here = first
        for x in range(XI):
            after = (last if x + 1 == XI - 1 else layer(ref, x + 1)) if x < XI - 1 else wrap
            yield x, (before, here, after)
            before, here = here, after

    for x in range(XI):
        for a in range(A):
            KP[x * A + a, inner, :] = arrange(GK, x, a)
    for x, fields in columns(KP):
        for a in range(A):
            k0 = fields[1][a]
            near = list(neighbours(KP, x, a, fields))
            outside = {}
            if x == 0:
                outside[0] = block == 0
            if x == XI - 1:
                outside[1] = block == Q - 1
            if a == 0:
                outside[4] = z_lo
            if a == A - 1:
                outside[5] = z_hi
            for q, mask in outside.items():
                near[q] = jnp.where(mask, 0.0, near[q])
            total = 2.0 * (6.0 * k0 + (((near[0] + near[1]) + (near[2] + near[3])) + (near[4] + near[5])))
            inv = RELAX / total
            for q in range(6):
                w = 2.0 * (k0 + near[q]) * inv
                if q in outside:
                    w = jnp.where(outside[q], 0.0, w)
                wts[q, x * A + a] = w
            wts[6, x * A + a] = inv

    for x in gb:
        x.wait_recv()
    eu1.start()
    eu1c.start()
    eu.start()
    euc.start()
    for x in range(XI):
        for a in range(A):
            i = x * A + a
            const = wts[6, i] * arrange(GB, x, a)
            wts[6, i] = const
            va[i, inner, :] = const

    def coarse_sweep(src, dst):
        for x, fields in columns(src):
            for a in range(A):
                i = x * A + a
                near = neighbours(src, x, a, fields)
                acc = [wts[q, i] * near[q] for q in range(6)]
                dst[i, inner, :] = (
                    ((acc[0] + acc[1]) + (acc[2] + acc[3]))
                    + ((acc[4] + acc[5]) + (KEEP * fields[1][a] + wts[6, i]))
                )

    @pl.loop(0, (ITERS_C - 1) // 2)
    def _(t):
        coarse_sweep(va, vb)
        coarse_sweep(vb, va)

    coarse_sweep(va, vb)

    eu1.wait_recv()
    eu1c.receive()
    grow_low = [
        select_matrix(mcols, mcols, lambda r, q, p=p: (q // 2 == cell(r)) & (r // (A * zw) == p))
        for p in range(2)
    ]
    window = crows + 2 * PAD
    rows_low = select_matrix(MY, window, lambda r, q: (r == 2 * (q - PAD // 2)) | (r == 2 * (q - PAD // 2) + 1))
    wide_block = lax.broadcasted_iota(jnp.int32, (window, mcols), 1) // zw

    def own_pair(n):
        t = s + n - 1
        at = lax.rem(t + S, S)
        q = at // (S // Q)
        x = 2 * lax.rem(at, S // Q)
        out = jnp.zeros((window, mcols), F32)
        for e in range(2):
            for a in range(A):
                group = e * A + a
                v = vb[(x + e) * A + a, pl.ds(pl.multiple_of(c * crows, crows), window), :]
                v = pltpu.roll(v, lax.rem(group - q + Q, Q) * zw, 1)
                out = jnp.where((wide_block == group) & (t >= 0) & (t < S), v, out)
        return out

    tall = jnp.concatenate([dot(rows_low, own_pair(n)) for n in range(3)], axis=0)
    for p in range(2):
        grown = dot(tall, grow_low[p])
        for n in range(3):
            for e in range(2):
                i = 4 * n + 2 * p + e
                U1[i] = UE1[i] + grown[n * MY:(n + 1) * MY]
    sweep(K1, F1, B1, W1, U1, V1, 1.0, range(HM - 3, HM + mdepth + 3))
    sweep(K1, F1, B1, W1, V1, U1, 1.0, range(HM - 2, HM + mdepth + 2))

    eu.wait_recv()
    euc.receive()
    grow_z = select_matrix(mcols, cols, lambda r, q: (q == 2 * r) | (q == 2 * r + 1))
    rows_mid = select_matrix(FY, MY, lambda r, q: (r == 2 * (q - PAD // 2)) | (r == 2 * (q - PAD // 2) + 1))
    mids = range(HM - 2, HM + mdepth + 2)
    all_grown = dot(jnp.concatenate([dot(rows_mid, U1[m]) for m in mids], axis=0), grow_z)
    for q, m in enumerate(mids):
        grown = all_grown[q * FY:(q + 1) * FY]
        for i in (2 * (m - HM) + HF, 2 * (m - HM) + HF + 1):
            if 0 <= i < depth + 2 * HF:
                V[i] = UE[i] + grown
    sweep(K, FF, B, W, V, U, 0.5, range(HF - 2, HF + depth + 2))
    sweep(K, FF, B, W, U, V, 0.5, range(HF - 1, HF + depth + 1))

    for j in range(depth):
        i = HF + j
        p_out[j] = V[i, own, :]
        r_out[j] = fine_residual(i)[PAD:PAD + rows]

    for e in (ek, eb, ec, ek1, ek1c, eb1, eb1c, eu1, eu1c, eu, euc):
        e.wait_send()
    for x in gk + gb:
        x.wait_send()


def hand_over(p_in, r_in, p_out, r_out, sems):
    copies = [
        pltpu.make_async_copy(p_in, p_out, sems.at[0]),
        pltpu.make_async_copy(r_in, r_out, sems.at[1]),
    ]
    for x in copies:
        x.start()
    for x in copies:
        x.wait()


def local(S, C, divergence, inverse_density):
    depth, rows, cols = divergence.shape
    mdepth, mrows, mcols = depth // 2, rows // 2, cols // 2
    crows = mrows // 2
    fine = pltpu.VMEM((depth + 2 * HF, rows + 2 * PAD, cols), F32)
    mid = pltpu.VMEM((mdepth + 2 * HM, mrows + 2 * PAD, mcols), F32)
    low = pltpu.VMEM((S, crows * C, mcols), F32)
    wide = pltpu.VMEM((S, crows * C + 2 * PAD, mcols), F32)
    n = len(DIRS)
    peers = S * C - 1
    dma = pltpu.SemaphoreType.DMA
    out = jax.ShapeDtypeStruct(divergence.shape, F32)
    inner = pl.pallas_call(
        functools.partial(kernel, S, C),
        out_shape=(out, out),
        in_specs=[pl.BlockSpec(memory_space=pl.ANY)] * 2,
        out_specs=(pl.BlockSpec(memory_space=pltpu.VMEM),) * 2,
        scratch_shapes=[fine] * 7 + [mid] * 7 + [
            pltpu.VMEM((2, crows, mcols), F32), low, low, wide, wide, wide,
            pltpu.VMEM((7, S, crows * C, mcols), F32),
            pltpu.VMEM((mdepth * rows, cols), F32),
            pltpu.VMEM((mdepth * rows, mcols), F32),
            pltpu.VMEM((2, 4, 8, cols), F32), pltpu.VMEM((2, 4, 8, cols), F32),
            pltpu.VMEM((3, 4, 8, mcols), F32), pltpu.VMEM((3, 4, 8, mcols), F32),
            pltpu.VMEM((4,) + fine.shape, F32), pltpu.VMEM((4,) + mid.shape, F32),
            dma((2,)), dma((3, n)), dma((3, n)), dma((3, n)), dma((3, n)),
            dma((2, peers)), dma((2, peers)), dma((2, 4)), dma((2, 4)), dma((3, 4)), dma((3, 4)),
            pltpu.SemaphoreType.REGULAR((max(S, C).bit_length(),)),
        ],
        compiler_params=pltpu.CompilerParams(collective_id=0, has_side_effects=True),
    )(divergence, inverse_density)
    return pl.pallas_call(
        hand_over,
        out_shape=(out, out),
        in_specs=[pl.BlockSpec(memory_space=pltpu.VMEM)] * 2,
        out_specs=(pl.BlockSpec(memory_space=pl.ANY),) * 2,
        scratch_shapes=[dma((2,))],
    )(*inner)


def solution(mesh):
    placed = P("span", "cross", None)
    return jax.shard_map(
        functools.partial(local, mesh.shape["span"], mesh.shape["cross"]),
        mesh=mesh,
        in_specs=(placed, placed),
        out_specs=(placed, placed),
        check_vma=False,
    )
```

```python
import functools

import jax
import jax.numpy as jnp
from jax import lax
from jax.experimental import pallas as pl
from jax.experimental.pallas import tpu as pltpu
from jax.sharding import PartitionSpec as P

ITERS_C = 64
RELAX = 0.8
KEEP = 1.0 - RELAX
HF = 3
HM = 4
PAD = 8
Q = 4
A = Q // 2
MC = HM - 1
DIRS = [(dx, dy) for dx in (-1, 0, 1) for dy in (-1, 0, 1) if (dx, dy) != (0, 0)]
HI = lax.Precision.HIGHEST
F32 = jnp.float32


def dot(a, b):
    return jnp.dot(a, b, precision=HI, preferred_element_type=F32)


def select_matrix(rows, cols, test):
    r = lax.broadcasted_iota(jnp.int32, (rows, cols), 0)
    c = lax.broadcasted_iota(jnp.int32, (rows, cols), 1)
    return jnp.where(test(r, c), 1.0, 0.0).astype(F32)


def kernel(S, C, b_hbm, k_hbm, p_out, r_out,
           K, B, U, V, W, DD, UE, K1, B1, U1, V1, W1, D1, UE1,
           stage, GK, GB, KP, va, vb, wts, t256, t128,
           corner_out, corner_in, mid_out, mid_in, FF, F1,
           load_sem, send_f, recv_f, send_m, recv_m, send_g, recv_g, send_c, recv_c, send_k, recv_k, known):
    depth, rows, cols = b_hbm.shape
    FY = rows + 2 * PAD
    mdepth, mrows, mcols = depth // 2, rows // 2, cols // 2
    MY = mrows + 2 * PAD
    crows = mrows // 2
    CR = crows * C
    zw = mcols // Q
    XI = 2 * S // Q
    NV = XI * A
    s = lax.axis_index("span")
    c = lax.axis_index("cross")

    loads = [
        pltpu.make_async_copy(k_hbm, K.at[pl.ds(HF, depth), pl.ds(PAD, rows), :], load_sem.at[0]),
        pltpu.make_async_copy(b_hbm, B.at[pl.ds(HF, depth), pl.ds(PAD, rows), :], load_sem.at[1]),
    ]
    for x in loads:
        x.start()

    def peer(o):
        return (lax.rem(s + o[0], S), lax.rem(c + o[1], C))


    def exists(dx, dy):
        return (s + dx >= 0) & (s + dx < S) & (c + dy >= 0) & (c + dy < C)

    def greet(sem, step):
        for dx, dy in DIRS:
            @pl.when(exists(dx * step, dy * step))
            def _(dx=dx, dy=dy):
                pl.semaphore_signal(
                    sem, inc=1, device_id=(s + dx * step, c + dy * step), device_id_type=pl.DeviceIdType.MESH
                )

    def heard(sem, step):
        present = [jnp.where(exists(dx * step, dy * step), 1, 0) for dx, dy in DIRS]
        pl.semaphore_wait(sem, sum(present))

    barrier = pltpu.get_barrier_semaphore()
    greet(barrier, 1)

    def spans(dx, dy, halo, h0, h1, n, r):
        if dx == 0:
            sl, dl, ln = halo, halo, n
        elif dx == 1:
            sl, dl, ln = halo + n - h1, halo - h1, h1 - h0
        else:
            sl, dl, ln = halo + h0, halo + n + h0, h1 - h0
        if dy == 0:
            sr, dr, rn = PAD, PAD, r
        elif dy == 1:
            sr, dr, rn = PAD + r - PAD, 0, PAD
        else:
            sr, dr, rn = PAD, PAD + r, PAD
        return sl, dl, ln, sr, dr, rn

    class Exchange:
        def __init__(self, buf, halo, h0, h1, n, r, ssem, rsem, slot, source=None, corners=True, along=False):
            self.items = []
            for q, (dx, dy) in enumerate(DIRS):
                if (dx == 0 and h0 > 0 and not along) or (dx != 0 and dy != 0 and not corners):
                    continue
                sl, dl, ln, sr, dr, rn = spans(dx, dy, halo, h0, h1, n, r)
                if source is None:
                    src = buf.at[pl.ds(sl, ln), pl.ds(sr, rn), :]
                else:
                    src = source.at[pl.ds(sl - halo, ln), pl.ds(sr - PAD, rn), :]
                copy = pltpu.make_async_remote_copy(
                    src_ref=src,
                    dst_ref=buf.at[pl.ds(dl, ln), pl.ds(dr, rn), :],
                    send_sem=ssem.at[slot, q],
                    recv_sem=rsem.at[slot, q],
                    device_id=(jnp.clip(s + dx, 0, S - 1), jnp.clip(c + dy, 0, C - 1)),
                    device_id_type=pl.DeviceIdType.MESH,
                )
                self.items.append((dx, dy, copy))

        def start(self):
            for dx, dy, copy in self.items:
                @pl.when(exists(dx, dy))
                def _(copy=copy):
                    copy.start()

        def wait_recv(self, span=None):
            for dx, dy, copy in self.items:
                if span is not None and span != abs(dx):
                    continue

                @pl.when(exists(-dx, -dy))
                def _(copy=copy):
                    copy.wait_recv()

        def wait_send(self):
            for dx, dy, copy in self.items:
                @pl.when(exists(dx, dy))
                def _(copy=copy):
                    copy.wait_send()

    def zero_edges(buf, halo, n, r):
        total = buf.shape[1]
        width = buf.shape[2]

        @pl.when(s == 0)
        def _():
            buf[0:halo] = jnp.zeros((halo, total, width), F32)

        @pl.when(s == S - 1)
        def _():
            buf[halo + n:] = jnp.zeros((halo, total, width), F32)

        @pl.when(c == 0)
        def _():
            buf[:, 0:PAD, :] = jnp.zeros((n + 2 * halo, PAD, width), F32)

        @pl.when(c == C - 1)
        def _():
            buf[:, PAD + r:, :] = jnp.zeros((n + 2 * halo, PAD, width), F32)

    class Corners:
        def __init__(self, slot, bufs):
            self.slot, self.bufs, self.items = slot, bufs, []
            for q, (dx, dy) in enumerate((i, j) for i in (-1, 1) for j in (-1, 1)):
                copy = pltpu.make_async_remote_copy(
                    src_ref=corner_out.at[slot, q],
                    dst_ref=corner_in.at[slot, q],
                    send_sem=send_c.at[slot, q],
                    recv_sem=recv_c.at[slot, q],
                    device_id=(jnp.clip(s + dx, 0, S - 1), jnp.clip(c + dy, 0, C - 1)),
                    device_id_type=pl.DeviceIdType.MESH,
                )
                self.items.append((q, dx, dy, copy))

        def pack(self):
            for q, dx, dy, copy in self.items:
                at = 0
                for buf in self.bufs:
                    for e in range(2):
                        layer = HF + depth - 1 - e if dx == 1 else HF + e
                        row = PAD + rows - 2 if dy == 1 else PAD
                        corner_out[self.slot, q, at:at + 2, :] = buf[layer, row:row + 2, :]
                        at += 2

        def start(self):
            for q, dx, dy, copy in self.items:
                @pl.when(exists(dx, dy))
                def _(copy=copy):
                    copy.start()

        def receive(self):
            for q, dx, dy, copy in self.items:
                @pl.when(exists(-dx, -dy))
                def _(q=q, dx=dx, dy=dy, copy=copy):
                    copy.wait_recv()
                    at = 0
                    for buf in self.bufs:
                        for e in range(2):
                            layer = HF - 1 - e if dx == 1 else HF + depth + e
                            row = PAD - 2 if dy == 1 else PAD + rows
                            buf[layer, row:row + 2, :] = corner_in[self.slot, q, at:at + 2, :]
                            at += 2

        def wait_send(self):
            for q, dx, dy, copy in self.items:
                @pl.when(exists(dx, dy))
                def _(copy=copy):
                    copy.wait_send()

    class MidCorners:
        def __init__(self, slot, buf):
            self.slot, self.buf, self.items = slot, buf, []
            for q, (dx, dy) in enumerate((i, j) for i in (-1, 1) for j in (-1, 1)):
                copy = pltpu.make_async_remote_copy(
                    src_ref=mid_out.at[slot, q],
                    dst_ref=mid_in.at[slot, q],
                    send_sem=send_k.at[slot, q],
                    recv_sem=recv_k.at[slot, q],
                    device_id=(jnp.clip(s + dx, 0, S - 1), jnp.clip(c + dy, 0, C - 1)),
                    device_id_type=pl.DeviceIdType.MESH,
                )
                self.items.append((q, dx, dy, copy))

        def pack(self):
            for q, dx, dy, copy in self.items:
                at = 0
                for e in range(1, MC + 1):
                    n = MC + 1 - e
                    layer = HM + mdepth - e if dx == 1 else HM + e - 1
                    row = PAD + mrows - n if dy == 1 else PAD
                    mid_out[self.slot, q, at:at + n, :] = self.buf[layer, row:row + n, :]
                    at += n

        def start(self):
            for q, dx, dy, copy in self.items:
                @pl.when(exists(dx, dy))
                def _(copy=copy):
                    copy.start()

        def receive(self):
            for q, dx, dy, copy in self.items:
                @pl.when(exists(-dx, -dy))
                def _(q=q, dx=dx, dy=dy, copy=copy):
                    copy.wait_recv()
                    at = 0
                    for e in range(1, MC + 1):
                        n = MC + 1 - e
                        layer = HM - e if dx == 1 else HM + mdepth + e - 1
                        row = PAD - n if dy == 1 else PAD + mrows
                        self.buf[layer, row:row + n, :] = mid_in[self.slot, q, at:at + n, :]
                        at += n

        def wait_send(self):
            for q, dx, dy, copy in self.items:
                @pl.when(exists(dx, dy))
                def _(copy=copy):
                    copy.wait_send()

    corner_out[...] = jnp.zeros(corner_out.shape, F32)
    for buf in (K, B, UE):
        for i in (0, HF + depth):
            for j in (0, PAD + rows):
                buf[i:i + HF, j:j + PAD, :] = jnp.zeros((HF, PAD, cols), F32)
        zero_edges(buf, HF, depth, rows)
    mid_out[...] = jnp.zeros(mid_out.shape, F32)
    for buf, value in ((K1, 1.0), (B1, 0.0), (UE1, 0.0)):
        for i in (0, HM + mdepth):
            for j in (0, PAD + mrows):
                buf[i:i + HM, j:j + PAD, :] = jnp.full((HM, PAD, mcols), value, F32)
        zero_edges(buf, HM, mdepth, mrows)
    KP[...] = jnp.zeros(KP.shape, F32)
    va[...] = jnp.zeros(va.shape, F32)
    vb[...] = jnp.zeros(vb.shape, F32)

    heard(barrier, 1)
    steps = []
    while 2 ** len(steps) < max(S, C) - 1:
        steps.append(2 ** len(steps))
    pending = list(enumerate(steps))

    def meet(rounds):
        for _ in range(min(rounds, len(pending))):
            turn, step = pending.pop(0)
            heard(known.at[turn], step)
            if pending:
                greet(known.at[pending[0][0]], pending[0][1])

    greet(known.at[0], steps[0])
    ek = Exchange(K, HF, 0, 3, depth, rows, send_f, recv_f, 0, k_hbm, corners=False)
    eb = Exchange(B, HF, 0, 2, depth, rows, send_f, recv_f, 1, b_hbm, corners=False)
    ek.start()
    eb.start()
    for x in loads:
        x.wait()
    ec = Corners(0, (K, B))
    ec.pack()
    ec.start()

    pair_z = select_matrix(cols, mcols, lambda r, q: (r == 2 * q) | (r == 2 * q + 1))
    def cell(q):
        return (q % zw) * A + (q // zw) % A

    low = [
        select_matrix(mcols, mcols, lambda r, q, p=p: (r // 2 == cell(q)) & (q // (A * zw) == p))
        for p in range(2)
    ]

    def restrict_rows(n):
        return t128[pl.ds(0, n, stride=2), :] + t128[pl.ds(1, n, stride=2), :]

    def to_low(mid):
        n = (mdepth // 2) * mrows
        for j in range(mdepth // 2):
            t128[j * mrows:(j + 1) * mrows, :] = mid(2 * j) + mid(2 * j + 1)
        packed = restrict_rows(n // 2)
        return dot(packed[0:crows], low[0]) + dot(packed[crows:2 * crows], low[1])

    for j in range(mdepth):
        t256[j * rows:(j + 1) * rows, :] = (
            K[HF + 2 * j, pl.ds(PAD, rows), :] + K[HF + 2 * j + 1, pl.ds(PAD, rows), :]
        )
    t128[...] = dot(t256[...], pair_z)
    K1[HM:HM + mdepth, PAD:PAD + mrows, :] = (0.125 * restrict_rows(mdepth * mrows)).reshape(mdepth, mrows, mcols)
    ek1 = Exchange(K1, HM, 0, HM, mdepth, mrows, send_m, recv_m, 0, corners=False)
    ek1c = MidCorners(0, K1)
    ek1c.pack()
    ek1.start()
    ek1c.start()

    order = sorted(range(1, S), key=lambda i: (min(i, S - i), i))

    class Gather:
        def __init__(self, slot, dst):
            rows_c = pl.ds(pl.multiple_of(c * crows, crows), crows)

            def copy(src, at, n, where):
                return pltpu.make_async_remote_copy(
                    src_ref=src,
                    dst_ref=dst.at[at, rows_c, :],
                    send_sem=send_g.at[slot, n],
                    recv_sem=recv_g.at[slot, n],
                    device_id=where,
                    device_id_type=pl.DeviceIdType.MESH,
                )

            def onward(src, at, i):
                return [copy(src, at, S * j + i, peer((0, j))) for j in range(1, C)]

            own = stage.at[slot]
            self.far = {i: copy(own, s, i, peer((i, 0))) for i in order}
            self.near = {0: onward(own, s, 0)}
            for i in order:
                t = lax.rem(s - i + S, S)
                self.near[i] = onward(dst.at[t, rows_c, :], t, i)

        def start(self):
            for i in reversed(order):
                self.far[i].start()
            for x in self.near[0]:
                x.start()

        def wait_recv(self):
            for i in order:
                self.far[i].wait_recv()
                for x in self.near[i]:
                    x.start()
            for i in [0] + order:
                for x in self.near[i]:
                    x.wait_recv()

        def wait_send(self):
            for i in order:
                self.far[i].wait_send()
            for i in [0] + order:
                for x in self.near[i]:
                    x.wait_send()

    def own_block(dst, value):
        dst[s, pl.ds(pl.multiple_of(c * crows, crows), crows), :] = value

    k2 = 0.125 * to_low(lambda j: K1[HM + j, pl.ds(PAD, mrows), :])
    stage[0] = k2
    gk = Gather(0, GK)
    own_block(GK, k2)

    def coupling(Kr, Fr, Vr, i):
        k0, v0 = Kr[i], Vr[i]
        n, m = v0.shape
        x = (k0 + Kr[i - 1]) * Vr[i - 1] + (k0 + Kr[i + 1]) * Vr[i + 1]
        y = Fr[0, i] * pltpu.roll(v0, 1, 0) + Fr[1, i] * pltpu.roll(v0, n - 1, 0)
        z = Fr[2, i] * pltpu.roll(v0, 1, 1) + Fr[3, i] * pltpu.roll(v0, m - 1, 1)
        return x + (y + z)

    def diagonal(Kr, Fr, i, factor, halo, n, r):
        k0 = Kr[i]
        height, m = k0.shape
        lane = lax.broadcasted_iota(jnp.int32, k0.shape, 1)
        y0, y1 = pltpu.roll(k0, 1, 0), pltpu.roll(k0, height - 1, 0)
        z0 = jnp.where(lane == 0, 0.0, pltpu.roll(k0, 1, 1))
        z1 = jnp.where(lane == m - 1, 0.0, pltpu.roll(k0, m - 1, 1))
        Fr[0, i] = k0 + y0
        Fr[1, i] = k0 + y1
        Fr[2, i] = jnp.where(lane == 0, 0.0, k0 + z0)
        Fr[3, i] = jnp.where(lane == m - 1, 0.0, k0 + z1)
        total = factor * (6.0 * k0 + ((Kr[i - 1] + Kr[i + 1]) + ((y0 + y1) + (z0 + z1))))
        y = lax.broadcasted_iota(jnp.int32, k0.shape, 0) + (c * r - PAD)
        inside = (y >= 0) & (y < r * C)
        x = s * n - halo + i
        xin = jnp.where((x >= 0) & (x < n * S), 1.0, 0.0).astype(F32)
        total = jnp.where(inside, total, 1.0) + (1.0 - xin)
        return total, jnp.where(inside, RELAX / total, 0.0) * xin

    def sweep(Kr, Fr, Br, Wr, src, dst, factor, layers):
        for i in layers:
            dst[i] = KEEP * src[i] + Wr[i] * (Br[i] + factor * coupling(Kr, Fr, src, i))

    def split(lo, hi, inner_lo, inner_hi):
        return list(range(inner_lo, inner_hi)), [i for i in range(lo, hi) if not inner_lo <= i < inner_hi]

    def fine_start(layers):
        for i in layers:
            total, inv = diagonal(K, FF, i, 0.5, HF, depth, rows)
            DD[i] = total
            W[i] = inv
            U[i] = B[i] * inv

    own = pl.ds(PAD, rows)

    def fine_residual(i):
        return B[i] - DD[i] * V[i] + 0.5 * coupling(K, FF, V, i)

    def fine_pairs(pairs):
        for j in pairs:
            i = HF + 2 * j
            both = fine_residual(i) + fine_residual(i + 1)
            t256[j * rows:(j + 1) * rows, :] = both[PAD:PAD + rows]

    end = HF + depth
    in_d, out_d = split(HF - 2, end + 2, HF + 1, end - 1)
    in_u, out_u = split(HF - 1, end + 1, HF + 2, end - 2)
    in_r, out_r = split(0, mdepth, 2, mdepth - 2)
    meet(1)
    ek.wait_recv(0)
    eb.wait_recv(0)
    fine_start(in_d)
    sweep(K, FF, B, W, U, V, 0.5, in_u)
    fine_pairs(in_r)
    ek.wait_recv(1)
    eb.wait_recv(1)
    ec.receive()
    meet(1)
    fine_start(out_d)
    sweep(K, FF, B, W, U, V, 0.5, out_u)
    fine_pairs(out_r)

    t128[...] = dot(t256[...], pair_z)
    B1[HM:HM + mdepth, PAD:PAD + mrows, :] = restrict_rows(mdepth * mrows).reshape(mdepth, mrows, mcols)
    eb1 = Exchange(B1, HM, 0, MC, mdepth, mrows, send_m, recv_m, 1, corners=False)
    eb1.start()
    eb1c = MidCorners(1, B1)
    eb1c.pack()
    eb1c.start()
    meet(len(steps))
    gk.start()

    UE[HF - 1:HF + depth + 1, PAD:PAD + rows, :] = V[HF - 1:HF + depth + 1, PAD:PAD + rows, :]
    ek1.wait_recv()
    ek1c.receive()

    for i in range(HM - 3, HM + mdepth + 3):
        total, inv = diagonal(K1, F1, i, 1.0, HM, mdepth, mrows)
        D1[i] = total
        W1[i] = inv

    eb1.wait_recv()
    eb1c.receive()
    for i in range(HM - 2, HM + mdepth + 2):
        U1[i] = W1[i] * B1[i]
    sweep(K1, F1, B1, W1, U1, V1, 1.0, range(HM - 1, HM + mdepth + 1))

    def mid_residual(j):
        i = HM + j
        return (B1[i] - D1[i] * V1[i] + coupling(K1, F1, V1, i))[PAD:PAD + mrows]

    b2 = to_low(mid_residual)
    stage[1] = b2
    gb = Gather(1, GB)
    gb.start()
    own_block(GB, b2)

    UE1[HM - 1:HM + mdepth + 1, PAD:PAD + mrows, :] = V1[HM - 1:HM + mdepth + 1, PAD:PAD + mrows, :]
    eu1 = Exchange(UE1, HM, 1, HM, mdepth, mrows, send_m, recv_m, 2, corners=False, along=True)
    eu1c = MidCorners(2, UE1)
    eu1c.pack()
    eu = Exchange(UE, HF, 1, HF, depth, rows, send_f, recv_f, 2, corners=False, along=True)
    euc = Corners(1, (UE,))
    euc.pack()

    gk.wait_recv()
    inner = pl.ds(PAD, CR)
    lane = lax.broadcasted_iota(jnp.int32, (CR, mcols), 1)
    block = lane // zw
    z_lo = lane % zw == 0
    z_hi = lane % zw == zw - 1

    def arrange(src, x, a):
        group = (x % 2) * A + a
        out = None
        for q in range(Q):
            v = src[q * (S // Q) + x // 2]
            if q != group:
                v = pltpu.roll(v, ((q - group) * zw) % mcols, 1)
            out = v if out is None else jnp.where(block == q, v, out)
        return out

    def neighbours(ref, x, a, fields):
        before, here, after = fields
        i = x * A + a
        return (
            before[a],
            after[a],
            ref[i, pl.ds(PAD - 1, CR), :],
            ref[i, pl.ds(PAD + 1, CR), :],
            here[a - 1] if a > 0 else pltpu.roll(here[A - 1], 1, 1),
            here[a + 1] if a < A - 1 else pltpu.roll(here[0], mcols - 1, 1),
        )

    def layer(ref, x):
        return [ref[x * A + a, inner, :] for a in range(A)]

    def columns(ref):
        first, last = layer(ref, 0), layer(ref, XI - 1)
        before = [pltpu.roll(v, zw, 1) for v in last]
        wrap = [pltpu.roll(v, mcols - zw, 1) for v in first]
        here = first
        for x in range(XI):
            after = (last if x + 1 == XI - 1 else layer(ref, x + 1)) if x < XI - 1 else wrap
            yield x, (before, here, after)
            before, here = here, after

    for x in range(XI):
        for a in range(A):
            KP[x * A + a, inner, :] = arrange(GK, x, a)
    for x, fields in columns(KP):
        for a in range(A):
            k0 = fields[1][a]
            near = list(neighbours(KP, x, a, fields))
            outside = {}
            if x == 0:
                outside[0] = block == 0
            if x == XI - 1:
                outside[1] = block == Q - 1
            if a == 0:
                outside[4] = z_lo
            if a == A - 1:
                outside[5] = z_hi
            for q, mask in outside.items():
                near[q] = jnp.where(mask, 0.0, near[q])
            total = 2.0 * (6.0 * k0 + (((near[0] + near[1]) + (near[2] + near[3])) + (near[4] + near[5])))
            inv = RELAX / total
            for q in range(6):
                w = 2.0 * (k0 + near[q]) * inv
                if q in outside:
                    w = jnp.where(outside[q], 0.0, w)
                wts[q, x * A + a] = w
            wts[6, x * A + a] = inv

    gb.wait_recv()
    eu1.start()
    eu1c.start()
    eu.start()
    euc.start()
    for x in range(XI):
        for a in range(A):
            i = x * A + a
            const = wts[6, i] * arrange(GB, x, a)
            wts[6, i] = const
            va[i, inner, :] = const

    def coarse_sweep(src, dst):
        for x, fields in columns(src):
            for a in range(A):
                i = x * A + a
                near = neighbours(src, x, a, fields)
                acc = [wts[q, i] * near[q] for q in range(6)]
                dst[i, inner, :] = (
                    ((acc[0] + acc[1]) + (acc[2] + acc[3]))
                    + ((acc[4] + acc[5]) + (KEEP * fields[1][a] + wts[6, i]))
                )

    @pl.loop(0, (ITERS_C - 1) // 2)
    def _(t):
        coarse_sweep(va, vb)
        coarse_sweep(vb, va)

    coarse_sweep(va, vb)

    eu1.wait_recv()
    eu1c.receive()
    grow_low = [
        select_matrix(mcols, mcols, lambda r, q, p=p: (q // 2 == cell(r)) & (r // (A * zw) == p))
        for p in range(2)
    ]
    window = crows + 2 * PAD
    rows_low = select_matrix(MY, window, lambda r, q: (r == 2 * (q - PAD // 2)) | (r == 2 * (q - PAD // 2) + 1))
    wide_block = lax.broadcasted_iota(jnp.int32, (window, mcols), 1) // zw

    def own_pair(n):
        t = s + n - 1
        at = lax.rem(t + S, S)
        q = at // (S // Q)
        x = 2 * lax.rem(at, S // Q)
        out = jnp.zeros((window, mcols), F32)
        for e in range(2):
            for a in range(A):
                group = e * A + a
                v = vb[(x + e) * A + a, pl.ds(pl.multiple_of(c * crows, crows), window), :]
                v = pltpu.roll(v, lax.rem(group - q + Q, Q) * zw, 1)
                out = jnp.where((wide_block == group) & (t >= 0) & (t < S), v, out)
        return out

    tall = jnp.concatenate([dot(rows_low, own_pair(n)) for n in range(3)], axis=0)
    for p in range(2):
        grown = dot(tall, grow_low[p])
        for n in range(3):
            for e in range(2):
                i = 4 * n + 2 * p + e
                U1[i] = UE1[i] + grown[n * MY:(n + 1) * MY]
    sweep(K1, F1, B1, W1, U1, V1, 1.0, range(HM - 3, HM + mdepth + 3))
    sweep(K1, F1, B1, W1, V1, U1, 1.0, range(HM - 2, HM + mdepth + 2))

    eu.wait_recv()
    euc.receive()
    grow_z = select_matrix(mcols, cols, lambda r, q: (q == 2 * r) | (q == 2 * r + 1))
    rows_mid = select_matrix(FY, MY, lambda r, q: (r == 2 * (q - PAD // 2)) | (r == 2 * (q - PAD // 2) + 1))
    mids = range(HM - 2, HM + mdepth + 2)
    all_grown = dot(jnp.concatenate([dot(rows_mid, U1[m]) for m in mids], axis=0), grow_z)
    for q, m in enumerate(mids):
        grown = all_grown[q * FY:(q + 1) * FY]
        for i in (2 * (m - HM) + HF, 2 * (m - HM) + HF + 1):
            if 0 <= i < depth + 2 * HF:
                V[i] = UE[i] + grown
    sweep(K, FF, B, W, V, U, 0.5, range(HF - 2, HF + depth + 2))
    sweep(K, FF, B, W, U, V, 0.5, range(HF - 1, HF + depth + 1))

    for j in range(depth):
        i = HF + j
        p_out[j] = V[i, own, :]
        r_out[j] = fine_residual(i)[PAD:PAD + rows]

    for e in (ek, eb, ec, ek1, ek1c, eb1, eb1c, eu1, eu1c, eu, euc):
        e.wait_send()
    gk.wait_send()
    gb.wait_send()


def hand_over(p_in, r_in, p_out, r_out, sems):
    copies = [
        pltpu.make_async_copy(p_in, p_out, sems.at[0]),
        pltpu.make_async_copy(r_in, r_out, sems.at[1]),
    ]
    for x in copies:
        x.start()
    for x in copies:
        x.wait()


def local(S, C, divergence, inverse_density):
    depth, rows, cols = divergence.shape
    mdepth, mrows, mcols = depth // 2, rows // 2, cols // 2
    crows = mrows // 2
    fine = pltpu.VMEM((depth + 2 * HF, rows + 2 * PAD, cols), F32)
    mid = pltpu.VMEM((mdepth + 2 * HM, mrows + 2 * PAD, mcols), F32)
    low = pltpu.VMEM((S, crows * C, mcols), F32)
    wide = pltpu.VMEM((S, crows * C + 2 * PAD, mcols), F32)
    n = len(DIRS)
    peers = S * C
    dma = pltpu.SemaphoreType.DMA
    out = jax.ShapeDtypeStruct(divergence.shape, F32)
    inner = pl.pallas_call(
        functools.partial(kernel, S, C),
        out_shape=(out, out),
        in_specs=[pl.BlockSpec(memory_space=pl.ANY)] * 2,
        out_specs=(pl.BlockSpec(memory_space=pltpu.VMEM),) * 2,
        scratch_shapes=[fine] * 7 + [mid] * 7 + [
            pltpu.VMEM((2, crows, mcols), F32), low, low, wide, wide, wide,
            pltpu.VMEM((7, S, crows * C, mcols), F32),
            pltpu.VMEM((mdepth * rows, cols), F32),
            pltpu.VMEM((mdepth * rows, mcols), F32),
            pltpu.VMEM((2, 4, 8, cols), F32), pltpu.VMEM((2, 4, 8, cols), F32),
            pltpu.VMEM((3, 4, 8, mcols), F32), pltpu.VMEM((3, 4, 8, mcols), F32),
            pltpu.VMEM((4,) + fine.shape, F32), pltpu.VMEM((4,) + mid.shape, F32),
            dma((2,)), dma((3, n)), dma((3, n)), dma((3, n)), dma((3, n)),
            dma((2, peers)), dma((2, peers)), dma((2, 4)), dma((2, 4)), dma((3, 4)), dma((3, 4)),
            pltpu.SemaphoreType.REGULAR((max(S, C).bit_length(),)),
        ],
        compiler_params=pltpu.CompilerParams(collective_id=0, has_side_effects=True),
    )(divergence, inverse_density)
    return pl.pallas_call(
        hand_over,
        out_shape=(out, out),
        in_specs=[pl.BlockSpec(memory_space=pltpu.VMEM)] * 2,
        out_specs=(pl.BlockSpec(memory_space=pl.ANY),) * 2,
        scratch_shapes=[dma((2,))],
    )(*inner)


def solution(mesh):
    placed = P("span", "cross", None)
    return jax.shard_map(
        functools.partial(local, mesh.shape["span"], mesh.shape["cross"]),
        mesh=mesh,
        in_specs=(placed, placed),
        out_specs=(placed, placed),
        check_vma=False,
    )
```
